256 devices in a mesh: section: 2 (over x_lo), ctx: 128 (over x_hi, y, z, core).
Axes of the slice: x: 4 (x_hi: 2, x_lo: 2; x = x_hi * 2 + x_lo), y: 4, z: 8, core: 2. Of those that a mesh axis runs over, the one named last changes fastest.
Arguments:
- query_rows: bfloat16 [2, 16384, 1536], P('section', 'ctx'), may hold values from -5 to 5
- key_rows: bfloat16 [2, 16384, 1536], P('section', 'ctx'), may hold values from -5 to 5
- value_rows: bfloat16 [2, 16384, 1536], P('section', 'ctx'), may hold values from -6 to 6
- grad_output: bfloat16 [2, 16384, 1536], P('section', 'ctx'), may hold values from -6 to 6
- block_lists: int32 [128, 5], P('ctx'), may hold values from -1 to 127, as said below
Outputs:
- grad_query: bfloat16 [2, 16384, 1536], P('section', 'ctx')
- grad_key: bfloat16 [2, 16384, 1536], P('section', 'ctx')
- grad_value: bfloat16 [2, 16384, 1536], P('section', 'ctx')
- handoff: bfloat16 [2, 16384, 1536], P('section', 'ctx')
The draws below stay inside these ranges and needn't reach their ends.
Inputs may be any that keep to these rules, and one draw needn't show every extreme that they name: `block_lists`: each list names distinct key blocks whose devices lie within 2 devices of the query block's device, always including the query block itself; -1 marks an unused entry; in every draw some query block names all 5 blocks.
All inputs are finite; a program needn't handle non-finite values.
Results may differ from the reference program's by a relative error of at most 0.011.
Values may be sent and summed in bfloat16 or wider, within the bound.
A program may use at most 128 MiB of HBM per device.

```python
import jax
import jax.numpy as jnp
from jax import lax

H = 12
DH = 128
BLK = 128
BPD = 1
REACH = 2
HD = 1536
NBLK = 128
SEQ = 16384
MAXN = 5
SECTIONS = 2


def query_key_pair(key):
    shape = (SECTIONS, NBLK, BLK, HD)
    first = jax.random.fold_in(key, 701)
    second = jax.random.fold_in(key, 702)
    queries = jnp.clip(jax.random.normal(first, shape, jnp.float32), -4.5, 4.5)
    keys_all = jnp.clip(jax.random.normal(second, shape, jnp.float32), -4.5, 4.5)
    return (queries.reshape(SECTIONS, SEQ, HD), keys_all.reshape(SECTIONS, SEQ, HD))


def draw_query_rows(key, part):
    return query_key_pair(key)[0].astype(jnp.bfloat16)


def draw_key_rows(key, part):
    return query_key_pair(key)[1].astype(jnp.bfloat16)


def draw_block_lists(key, part):
    devices_all = NBLK // BPD
    query_block = jnp.arange(NBLK).reshape(NBLK, 1)
    query_device = query_block // BPD
    column = jnp.arange(MAXN).reshape(1, MAXN)
    distance = column // BPD - REACH
    within = column % BPD
    candidate = (query_device + distance) * BPD + within
    inside = (candidate >= 0) & (candidate < NBLK)
    rolled = jax.random.randint(jax.random.fold_in(key, 801), (NBLK, MAXN), 0, 100)
    keep = rolled < 100 - 15 * jnp.abs(distance)
    full_device = jax.random.randint(jax.random.fold_in(key, 802), (), REACH, devices_all - REACH)
    full_block = full_device * BPD + jax.random.randint(jax.random.fold_in(key, 803), (), 0, BPD)
    keep = keep | (candidate == query_block) | (query_block == full_block)
    return jnp.where(inside & keep, candidate, -1).astype(jnp.int32)


def shard_levels(key, shape, pieces, low, largest):
    level = 1.0
    for dim, blocks in pieces:
        heights = jax.random.uniform(jax.random.fold_in(jax.random.fold_in(key, 6), dim), (blocks,), jnp.float32, low / len(pieces), largest / len(pieces))
        level = level * jnp.repeat(jnp.exp(heights), shape[dim] // blocks).reshape((-1,) + (1,) * (len(shape) - 1 - dim))
    return level


def scatter_about(rng, shape, scale, bound, split=(), dtype=jnp.bfloat16):
    loudness = shard_levels(rng, shape, split, -0.22, 0.18) if split else 1.0
    result = jax.random.normal(rng, shape, jnp.float32) * scale * loudness
    return jnp.minimum(jnp.maximum(result, -bound), bound).astype(dtype)


def setup_inputs(seed: int = 0) -> dict:
    streams_of = jax.random.split(jax.random.key(seed), 6)
    return {
        "query_rows": draw_query_rows(jax.random.fold_in(streams_of[5], 71), 0),
        "key_rows": draw_key_rows(jax.random.fold_in(streams_of[5], 71), 0),
        "value_rows": scatter_about(streams_of[2], (SECTIONS, SEQ, HD), 1.0, 6.0, ((0, 2), (1, 128))),
        "grad_output": scatter_about(streams_of[3], (SECTIONS, SEQ, HD), 1.0, 6.0, ((0, 2), (1, 128))),
        "block_lists": draw_block_lists(jax.random.fold_in(streams_of[5], 71), 0),
    }


big_negative = -1.0e30


def layer_grads(query_rows, key_rows, value_rows, grad_output, block_lists):
    scale = DH ** -0.5
    blocks = block_lists.shape[0]
    query_blocks = query_rows.reshape(blocks, BLK, H, DH)
    key_blocks = key_rows.reshape(blocks, BLK, H, DH)
    value_blocks = value_rows.reshape(blocks, BLK, H, DH)
    grad_blocks = grad_output.reshape(blocks, BLK, H, DH)

    def visit(carry, inputs):
        key_acc, value_acc = carry
        query_one, grad_one, listed = inputs
        usable = listed >= 0
        picked = jnp.maximum(listed, 0).astype(jnp.int32)
        keys_here = key_blocks[picked].astype(jnp.float32)
        values_here = value_blocks[picked].astype(jnp.float32)
        query_full = query_one.astype(jnp.float32)
        grad_full = grad_one.astype(jnp.float32)
        scores = jnp.einsum("qhd,nkhd->hqnk", query_full, keys_here) * scale
        scores = jnp.where(usable[None, None, :, None], scores, big_negative)
        highest = jnp.max(scores, axis=(2, 3), keepdims=True)
        weights = jnp.exp(scores - highest)
        probs = weights / jnp.sum(weights, axis=(2, 3), keepdims=True)
        probs_back = lax.optimization_barrier(probs.astype(jnp.bfloat16)).astype(jnp.float32)
        attended = jnp.einsum("hqnk,nkhd->qhd", probs_back, values_here)
        delta = jnp.sum(grad_full * attended, axis=2)
        value_part = jnp.einsum("hqnk,qhd->nkhd", probs_back, grad_full)
        grad_probs = jnp.einsum("qhd,nkhd->hqnk", grad_full, values_here)
        grad_scores = probs * (grad_probs - jnp.transpose(delta)[:, :, None, None])
        scores_back = lax.optimization_barrier(grad_scores.astype(jnp.bfloat16)).astype(jnp.float32)
        query_part = jnp.einsum("hqnk,nkhd->qhd", scores_back, keys_here) * scale
        key_part = jnp.einsum("hqnk,qhd->nkhd", scores_back, query_full) * scale
        key_acc = key_acc.at[picked].add(key_part)
        value_acc = value_acc.at[picked].add(value_part)
        return (key_acc, value_acc), query_part

    empty = jnp.zeros((blocks, BLK, H, DH), jnp.float32)
    (key_acc, value_acc), query_grads = lax.scan(visit, (empty, empty), (query_blocks, grad_blocks, block_lists))
    total = blocks * BLK
    width = H * DH
    return (query_grads.reshape(total, width).astype(jnp.bfloat16),
            key_acc.reshape(total, width).astype(jnp.bfloat16),
            value_acc.reshape(total, width).astype(jnp.bfloat16))


def reference(query_rows, key_rows, value_rows, grad_output, block_lists):
    query_list = []
    key_list = []
    value_list = []
    for layer in range(SECTIONS):
        grad_q, grad_k, grad_v = layer_grads(query_rows[layer], key_rows[layer], value_rows[layer], grad_output[layer], block_lists)
        query_list.append(grad_q)
        key_list.append(grad_k)
        value_list.append(grad_v)
    grad_query = jnp.stack(query_list)
    grad_key = jnp.stack(key_list)
    grad_value = jnp.stack(value_list)
    handoff = jnp.concatenate([grad_value[1:], jnp.zeros_like(grad_value[:1])], axis=0)
    return grad_query, grad_key, grad_value, handoff
```

```python
import functools

import jax
import jax.numpy as jnp
from jax import lax
from jax.experimental import pallas as pl
from jax.experimental.pallas import tpu as pltpu
from jax.sharding import PartitionSpec as P

H = 12
DH = 128
BLK = 128
REACH = 2
CORES = 2
SLOTS = H // CORES
ROWS = CORES * BLK
NEG = -1e30
MESH = pl.DeviceIdType.MESH
AHEAD = 2


def nt(a, b):
    return lax.dot_general(a, b, (((1,), (1,)), ((), ())), preferred_element_type=jnp.float32)


def nn(a, b):
    return lax.dot_general(a, b, (((1,), (0,)), ((), ())), preferred_element_type=jnp.float32)


def tn(a, b):
    return lax.dot_general(a, b, (((0,), (0,)), ((), ())), preferred_element_type=jnp.float32)


def kernel(
    chips,
    lists,
    q_hbm,
    k_hbm,
    v_hbm,
    g_hbm,
    dq_out,
    dk_out,
    dv_out,
    hand_out,
    own,
    near,
    mask_own,
    mask_chip,
    mask_near,
    e_buf,
    d_buf,
    stat_out,
    stat_own,
    stat_in,
    fac_out,
    fac_own,
    fac_in,
    dq_own,
    dq_send,
    dq_recv,
    stage,
    local_sem,
    part_send,
    part_recv,
    near_send,
    near_recv,
    mask_send,
    mask_recv,
    mask_part,
    stat_send,
    stat_recv,
    fac_send,
    fac_recv,
    dq_ssem,
    dq_rsem,
    out_send,
    out_recv,
    hand_send,
    hand_recv,
):
    section = lax.axis_index("section")
    me = lax.axis_index("ctx")
    chip = me // CORES
    core = lax.rem(me, CORES)
    other = 1 - core
    partner = CORES * chip + other
    below = lax.rem(chip + chips - 1, chips)
    above = lax.rem(chip + 1, chips)
    sides = (below, above)
    scale = DH ** (-0.5)
    inputs = (q_hbm, g_hbm, k_hbm, v_hbm)
    mine = pl.ds(pl.multiple_of(core * BLK, BLK), BLK)
    theirs = pl.ds(pl.multiple_of(other * BLK, BLK), BLK)

    def columns(half, slot):
        return pl.ds(pl.multiple_of((half * SLOTS + slot) * DH, DH), DH)

    def ctx(index):
        return {"ctx": index}

    def load_local(slot, carry):
        for n, ref in enumerate(inputs):
            pltpu.make_async_copy(
                ref.at[0, :, columns(core, slot)], own.at[slot, n, mine, :], local_sem.at[slot]
            ).start()
        return carry

    lax.fori_loop(0, SLOTS, load_local, 0)

    row = lax.broadcasted_iota(jnp.int32, (8, BLK), 0)
    flags = jnp.zeros((8, BLK), jnp.float32)
    for step in range(2 * REACH + 1):
        named = jnp.float32(0)
        for n in range(2 * REACH + 1):
            entry = lists[0, n]
            hit = (entry == me + (step - REACH)) & (entry >= 0)
            named = jnp.maximum(named, jnp.where(hit, jnp.float32(1), jnp.float32(0)))
        flags = jnp.where(row == step, named, flags)
    mask_own[...] = flags

    barrier = pltpu.get_barrier_semaphore()
    greet = [{"ctx": partner}]
    greet += [{"ctx": CORES * side + d} for side in sides for d in range(CORES)]
    greet += [{"section": 1 - section, "ctx": CORES * chip + d} for d in range(CORES)]
    for device in greet:
        pl.semaphore_signal(barrier, inc=1, device_id=device, device_id_type=MESH)
    pl.semaphore_wait(barrier, len(greet))

    def remote(src, dst, ssem, rsem, device):
        return pltpu.make_async_remote_copy(
            src_ref=src, dst_ref=dst, send_sem=ssem, recv_sem=rsem, device_id=device, device_id_type=MESH
        )

    def arrived(ref, sem):
        pltpu.make_async_copy(ref, ref, sem).wait()

    for side in range(2):
        for d in range(CORES):
            remote(
                mask_own, mask_near.at[1 - side, core], mask_send.at[0], mask_recv.at[1 - side],
                ctx(CORES * sides[side] + d),
            ).start()
    remote(mask_own, mask_chip.at[core], mask_part.at[0], mask_part.at[1], ctx(partner)).start()
    mask_chip[core] = flags

    def send_near(slot):
        for side in range(2):
            for d in range(CORES):
                for n in range(2):
                    remote(
                        inputs[n].at[0, :, columns(d, slot)],
                        near.at[slot, 1 - side, n, mine, :],
                        near_send.at[slot],
                        near_recv.at[slot, 1 - side],
                        ctx(CORES * sides[side] + d),
                    ).start()

    def send_partner(slot):
        for n, ref in enumerate(inputs):
            remote(
                ref.at[0, :, columns(other, slot)],
                own.at[slot, n, mine, :],
                part_send.at[slot],
                part_recv.at[slot],
                ctx(partner),
            ).start()

    for slot in range(AHEAD):
        send_partner(slot)
        send_near(slot)
    for slot in range(AHEAD, SLOTS):
        send_partner(slot)

    @pl.when(section == 1)
    def _():
        hand_out[...] = jnp.zeros_like(hand_out)

    arrived(mask_near.at[0], mask_recv.at[0])
    arrived(mask_near.at[1], mask_recv.at[1])
    arrived(mask_chip.at[other], mask_part.at[1])

    def wanted(group, kb):
        parts = []
        for qb in range(CORES):
            step = kb - qb + REACH + CORES * (1 - group)
            if 0 <= step <= 2 * REACH:
                tile = mask_chip[qb] if group == 1 else mask_near[group // 2, qb]
                parts.append(tile[step : step + 1])
            else:
                parts.append(jnp.zeros((1, BLK), jnp.float32))
        return jnp.concatenate(parts, axis=1)

    def rows_of(slot, group, n):
        return own[slot, n] if group == 1 else near[slot, group // 2, n]

    def pack(first, *rest):
        rows = [first, *rest]
        pad = jnp.zeros((8 - len(rows), ROWS), jnp.float32)
        return jnp.concatenate([*rows, pad], axis=0)

    def step1(slot):
        arrived(own.at[slot, :, mine, :], local_sem.at[slot])
        arrived(own.at[slot, :, theirs, :], part_recv.at[slot])
        arrived(near.at[slot, 0], near_recv.at[slot, 0])
        arrived(near.at[slot, 1], near_recv.at[slot, 1])
        keys = own[slot, 2]
        values = own[slot, 3]
        for group in (0, 2, 1):
            scores = nt(keys, rows_of(slot, group, 0)) * scale
            halves = [
                jnp.where(wanted(group, kb) > 0, scores[kb * BLK : (kb + 1) * BLK], NEG)
                for kb in range(CORES)
            ]
            scores = jnp.concatenate(halves, axis=0)
            highest = jnp.max(scores, axis=0, keepdims=True)
            weights = jnp.exp(scores - highest)
            grad_probs = nt(values, rows_of(slot, group, 1))
            total = jnp.sum(weights, axis=0, keepdims=True)
            cross = jnp.sum(weights * grad_probs, axis=0, keepdims=True)
            e_buf[slot, group] = weights
            d_buf[slot, group] = grad_probs
            tile = pack(highest, total, cross)
            if group == 1:
                stat_own[slot] = tile
            else:
                side = group // 2
                stat_out[slot, side] = tile
                remote(
                    stat_out.at[slot, side], stat_in.at[slot, 1 - side],
                    stat_send.at[slot, side], stat_recv.at[slot, 1 - side],
                    ctx(CORES * sides[side] + core),
                ).start()

    def combine(slot):
        for side in range(2):
            arrived(stat_in.at[slot, side], stat_recv.at[slot, side])
        tiles = [stat_in[slot, 0], stat_own[slot], stat_in[slot, 1]]
        highest = jnp.maximum(jnp.maximum(tiles[0][0:1], tiles[1][0:1]), tiles[2][0:1])
        shrink = [jnp.exp(tile[0:1] - highest) for tile in tiles]
        denom = sum(tile[1:2] * s for tile, s in zip(tiles, shrink))
        delta = sum(tile[2:3] * s for tile, s in zip(tiles, shrink)) / denom
        for side in range(2):
            fac_out[slot, side] = pack(shrink[2 * side] / denom, delta)
            remote(
                fac_out.at[slot, side], fac_in.at[slot, 1 - side],
                fac_send.at[slot, side], fac_recv.at[slot, 1 - side],
                ctx(CORES * sides[side] + core),
            ).start()
        fac_own[slot] = pack(shrink[1] / denom, delta)

    def step2(slot):
        for side in range(2):
            arrived(fac_in.at[slot, side], fac_recv.at[slot, side])
        keys = own[slot, 2]
        key_grad = jnp.zeros((ROWS, DH), jnp.float32)
        value_grad = jnp.zeros((ROWS, DH), jnp.float32)
        for group in (0, 2, 1):
            tile = fac_own[slot] if group == 1 else fac_in[slot, group // 2]
            probs = e_buf[slot, group] * tile[0:1]
            probs_low = probs.astype(jnp.bfloat16)
            scores_low = (probs * (d_buf[slot, group] - tile[1:2])).astype(jnp.bfloat16)
            query_grad = tn(keys, scores_low) * scale
            if group == 1:
                dq_own[slot] = query_grad
            else:
                side = group // 2
                dq_send[slot, side] = query_grad.astype(jnp.bfloat16)
                remote(
                    dq_send.at[slot, side], dq_recv.at[slot, 1 - side],
                    dq_ssem.at[slot, side], dq_rsem.at[slot, 1 - side],
                    ctx(CORES * sides[side] + core),
                ).start()
            value_grad = value_grad + nn(probs_low, rows_of(slot, group, 1))
            key_grad = key_grad + nn(scores_low, rows_of(slot, group, 0))
        stage[slot, 1] = (key_grad * scale).astype(jnp.bfloat16)
        stage[slot, 2] = value_grad.astype(jnp.bfloat16)

        @pl.when(section == 1)
        def _():
            for b in range(CORES):
                remote(
                    stage.at[slot, 2, b * BLK : (b + 1) * BLK, :],
                    hand_out.at[0, :, columns(core, slot)],
                    hand_send.at[0],
                    hand_recv.at[0],
                    {"section": section - 1, "ctx": CORES * chip + b},
                ).start()

        for n, out in ((1, dk_out), (2, dv_out)):
            deliver(slot, n, out)

    def deliver(slot, n, out):
        remote(
            stage.at[slot, n, theirs, :],
            out.at[0, :, columns(core, slot)],
            out_send.at[0],
            out_recv.at[0],
            ctx(partner),
        ).start()
        out[0, :, columns(core, slot)] = stage[slot, n, mine, :]

    def final(slot):
        for side in range(2):
            arrived(dq_recv.at[slot, side], dq_rsem.at[slot, side])
        total = (
            dq_own[slot] + dq_recv[slot, 0].astype(jnp.float32) + dq_recv[slot, 1].astype(jnp.float32)
        )
        stage[slot, 0] = jnp.transpose(total).astype(jnp.bfloat16)
        deliver(slot, 0, dq_out)

    def turn(i, carry):
        @pl.when(i < SLOTS)
        def _():
            step1(i)

        @pl.when(i + AHEAD < SLOTS)
        def _():
            send_near(i + AHEAD)

        @pl.when((i >= 1) & (i < SLOTS + 1))
        def _():
            combine(i - 1)

        @pl.when((i >= 2) & (i < SLOTS + 2))
        def _():
            step2(i - 2)

        @pl.when((i >= 3) & (i < SLOTS + 3))
        def _():
            final(i - 3)

        return carry

    lax.fori_loop(0, SLOTS + 3, turn, 0)

    arrived(mask_near, mask_send.at[0])
    arrived(mask_own, mask_part.at[0])

    def drain(slot, carry):
        arrived(own.at[slot], near_send.at[slot])
        arrived(near.at[slot, 0], part_send.at[slot])
        for side in range(2):
            arrived(stat_out.at[slot, side], stat_send.at[slot, side])
            arrived(fac_out.at[slot, side], fac_send.at[slot, side])
            arrived(dq_send.at[slot, side], dq_ssem.at[slot, side])
        return carry

    lax.fori_loop(0, SLOTS, drain, 0)
    arrived(stage.at[:, :, mine, :], out_send.at[0])
    arrived(stage.at[:, :, mine, :], out_recv.at[0])

    @pl.when(section == 1)
    def _():
        arrived(hand_out, hand_send.at[0])

    @pl.when(section == 0)
    def _():
        arrived(hand_out, hand_recv.at[0])


def shards(query_rows, key_rows, value_rows, grad_output, block_lists):
    chips = lax.axis_size("ctx") // CORES
    shape = query_rows.shape
    low = jnp.bfloat16
    full = jnp.float32
    dma = pltpu.SemaphoreType.DMA
    any_spec = pl.BlockSpec(memory_space=pl.ANY)
    vmem_spec = pl.BlockSpec(memory_space=pltpu.VMEM)
    return pl.pallas_call(
        functools.partial(kernel, chips),
        out_shape=tuple(jax.ShapeDtypeStruct(shape, low) for _ in range(4)),
        in_specs=[pl.BlockSpec(memory_space=pltpu.SMEM)] + [any_spec] * 4,
        out_specs=tuple(vmem_spec for _ in range(4)),
        scratch_shapes=[
            pltpu.VMEM((SLOTS, 4, ROWS, DH), low),
            pltpu.VMEM((SLOTS, 2, 2, ROWS, DH), low),
            pltpu.VMEM((8, BLK), full),
            pltpu.VMEM((CORES, 8, BLK), full),
            pltpu.VMEM((2, CORES, 8, BLK), full),
            pltpu.VMEM((SLOTS, 3, ROWS, ROWS), full),
            pltpu.VMEM((SLOTS, 3, ROWS, ROWS), full),
            pltpu.VMEM((SLOTS, 2, 8, ROWS), full),
            pltpu.VMEM((SLOTS, 8, ROWS), full),
            pltpu.VMEM((SLOTS, 2, 8, ROWS), full),
            pltpu.VMEM((SLOTS, 2, 8, ROWS), full),
            pltpu.VMEM((SLOTS, 8, ROWS), full),
            pltpu.VMEM((SLOTS, 2, 8, ROWS), full),
            pltpu.VMEM((SLOTS, DH, ROWS), full),
            pltpu.VMEM((SLOTS, 2, DH, ROWS), low),
            pltpu.VMEM((SLOTS, 2, DH, ROWS), low),
            pltpu.VMEM((SLOTS, 3, ROWS, DH), low),
            dma((SLOTS,)),
            dma((SLOTS,)),
            dma((SLOTS,)),
            dma((SLOTS,)),
            dma((SLOTS, 2)),
            dma((1,)),
            dma((2,)),
            dma((2,)),
            dma((SLOTS, 2)),
            dma((SLOTS, 2)),
            dma((SLOTS, 2)),
            dma((SLOTS, 2)),
            dma((SLOTS, 2)),
            dma((SLOTS, 2)),
            dma((1,)),
            dma((1,)),
            dma((1,)),
            dma((1,)),
        ],
        compiler_params=pltpu.CompilerParams(collective_id=0, has_side_effects=True),
        name="attention_backward",
    )(block_lists, query_rows, key_rows, value_rows, grad_output)


def solution(mesh):
    spec = P("section", "ctx", None)
    return jax.shard_map(
        shards,
        mesh=mesh,
        in_specs=(spec, spec, spec, spec, P("ctx", None)),
        out_specs=(spec, spec, spec, spec),
        check_vma=False,
    )
```
